32 devices in a mesh: tile: 4 (over x, core), tm: 8 (over z, y).
Axes of the slice: x: 2, y: 2, z: 4, core: 2. Of those that a mesh axis runs over, the one named last changes fastest.
Arguments:
- ocean_heat_anomaly: bfloat16 [256, 96, 1024], P('tm', 'tile'), may hold values from -6 to 6
- observation_reliability: bfloat16 [256, 96, 1024], P('tm', 'tile'), may hold values from 0.099609375 to 1
- swath_date_number: int32 [256], replicated, may hold values from 0 to 255, as said below
- marine_cell_flag: int32 [96, 1024], P('tile'), may hold values 0 or 1
Outputs:
- trend: float32 [256, 96, 1024], P('tm', 'tile')
The draws below stay inside these ranges and needn't reach their ends.
Inputs may be any that keep to these rules, and one draw needn't show every extreme that they name: `swath_date_number`: every day appears exactly once; every index of tm holds the same number of granules of every block of 32 consecutive days, in no particular order.
All inputs are finite; a program needn't handle non-finite values. No bound on the sum of `marine_cell_flag` on one device may be relied on, other than what follows from the above.
Results may differ from the reference program's by a relative error of at most 0.0015.
Values may be sent and summed in bfloat16 or wider, within the bound.
No kernel may reach another device: no remote copies, remote signals or barrier semaphores. Data moves between devices by JAX's collectives and lax.ppermute only.
A program may use at most 128 MiB of HBM per device.

```python
import math
import jax
import jax.numpy as jnp
from jax import lax

DAYS_DEV = 32
GRID_WIDTH = 1024
DATE_COUNT = 256
GRID_HEIGHT = 96
N_TM = 8


def draw_swath_date_number(key, part):
    first_key, second_key = jax.random.split(jax.random.fold_in(key, 7))
    share = DAYS_DEV // N_TM
    days_grid = jnp.arange(DATE_COUNT, dtype=jnp.int32).reshape(N_TM, DAYS_DEV)
    block_perm = jax.vmap(lambda sub: jax.random.permutation(sub, DAYS_DEV))(jax.random.split(first_key, N_TM))
    chosen = jnp.take_along_axis(days_grid, block_perm.astype(jnp.int32), axis=1)
    chosen = chosen.reshape(N_TM, N_TM, share).transpose(1, 0, 2).reshape(N_TM, DAYS_DEV)
    source_perm = jax.vmap(lambda sub: jax.random.permutation(sub, DAYS_DEV))(jax.random.split(second_key, N_TM))
    shuffled = jnp.take_along_axis(chosen, source_perm.astype(jnp.int32), axis=1)
    return shuffled.reshape(DATE_COUNT).astype(jnp.int32)


def touch_ends(drawn, stream_key, smallest, largest):
    shape = drawn.shape
    index_at = [jax.random.randint(jax.random.fold_in(stream_key, axis), (), 0, shape[axis]) for axis in range(len(shape))]
    drawn = drawn.at[tuple(index_at)].set(smallest)
    longest = shape.index(max(shape))
    index_at[longest] = (index_at[longest] + 1) % shape[longest]
    return drawn.at[tuple(index_at)].set(largest)


def block_scale(rng, extent, cuts, least, high):
    def one(dim, shards_of):
        steps = jax.random.uniform(jax.random.fold_in(jax.random.fold_in(rng, 6), dim), (shards_of,), jnp.float32, least / len(cuts), high / len(cuts))
        return jnp.repeat(jnp.exp(steps), extent[dim] // shards_of).reshape((-1,) + (1,) * (len(extent) - dim - 1))

    gain = one(*cuts[0])
    for cut in cuts[1:]:
        gain = gain * one(*cut)
    return gain


def normal_values(rng, shape, spread, most, shards=(), held_as=jnp.bfloat16):
    values = jax.random.normal(rng, shape, jnp.float32) * spread
    if len(shards) > 0:
        values = block_scale(rng, shape, shards, -0.22, 0.18) * values
    return jnp.clip(values, min=-most, max=most).astype(held_as)


def setup_inputs(seed: int = 0) -> dict:
    seeds = jax.random.split(jax.random.key(seed), 5)
    ocean_heat_anomaly = normal_values(seeds[0], (DATE_COUNT, GRID_HEIGHT, GRID_WIDTH), 1.0, 6.0, ((0, 8), (1, 4)))
    observation_reliability = jnp.clip(jnp.exp(math.log(1.0) - 2.306499 * jax.random.uniform(seeds[1], (DATE_COUNT, GRID_HEIGHT, GRID_WIDTH), jnp.float32) ** block_scale(seeds[1], (DATE_COUNT, GRID_HEIGHT, GRID_WIDTH), ((0, 8), (1, 4)), -0.2, 0.2)), 0.099609375, 1.0).astype(jnp.bfloat16)
    swath_date_number = draw_swath_date_number(jax.random.fold_in(seeds[4], 71), 0)
    marine_cell_flag = touch_ends((jax.random.randint(seeds[3], (GRID_HEIGHT, GRID_WIDTH), 0, 4) < 3).astype(jnp.int32), jax.random.fold_in(seeds[3], 1), 0, 1)
    return dict(ocean_heat_anomaly=ocean_heat_anomaly, observation_reliability=observation_reliability, swath_date_number=swath_date_number, marine_cell_flag=marine_cell_flag)


DECAY = 0.999
UNIT = 256.0
RIDGE = 0.05


def slope_of(zeroth, first, second, level_sum, slope_sum, ocean):
    det = zeroth * (second + RIDGE) - first * first
    det = jnp.where(ocean > 0, det, jnp.float32(1.0))
    return (first * level_sum - zeroth * slope_sum) / det


def smooth(slopes, ocean):
    padded = jnp.pad(slopes, ((0, 0), (1, 1), (1, 1)))
    rowsum = padded[:, :-2] + padded[:, 1:-1] + padded[:, 2:]
    total = rowsum[:, :, :-2] + rowsum[:, :, 1:-1] + rowsum[:, :, 2:]
    mpad = jnp.pad(ocean, ((1, 1), (1, 1)))
    mrows = mpad[:-2] + mpad[1:-1] + mpad[2:]
    count = mrows[:, :-2] + mrows[:, 1:-1] + mrows[:, 2:]
    return total / jnp.maximum(count, 1.0)[None]


def reference(ocean_heat_anomaly, observation_reliability, swath_date_number, marine_cell_flag):
    ranking_positions = jnp.argsort(swath_date_number).astype(jnp.int32)
    ocean = marine_cell_flag.astype(jnp.float32)
    matrix_items = ocean_heat_anomaly[ranking_positions].astype(jnp.float32)
    weights = observation_reliability[ranking_positions].astype(jnp.float32) * ocean[None]
    step_size = 1.0 / UNIT

    def advance(state, inputs):
        weight_now, value_now = inputs
        zeroth, first, second, level_sum, slope_sum = state
        second = DECAY * (second + 2.0 * step_size * first + step_size * step_size * zeroth)
        first = DECAY * (first + step_size * zeroth)
        zeroth = DECAY * zeroth + weight_now
        slope_sum = DECAY * (slope_sum + step_size * level_sum)
        level_sum = DECAY * level_sum + weight_now * value_now
        slope = slope_of(zeroth, first, second, level_sum, slope_sum, ocean)
        return (zeroth, first, second, level_sum, slope_sum), slope

    empty = jnp.zeros(ocean.shape, jnp.float32)
    start = (empty, empty, empty, empty, empty)
    final_state, slopes = lax.scan(advance, start, (weights, matrix_items))
    return smooth(slopes, ocean)
```

```python
import functools
import math

import jax
import jax.numpy as jnp
from jax import lax
from jax.experimental import pallas as pl
from jax.experimental.pallas import tpu as pltpu
from jax.sharding import PartitionSpec as P

DECAY = 0.999
UNIT = 256.0
RIDGE = 0.05
TILE = 8
LANES = 512


SMEM = pl.BlockSpec(memory_space=pltpu.SMEM)
VMEM = pl.BlockSpec(memory_space=pltpu.VMEM)
STEP = 1.0 / UNIT


def shifted(state, factor, offset):
    zeroth, first, second, level_sum, slope_sum = state
    return (
        factor * zeroth,
        factor * (first + offset * zeroth),
        factor * (second + 2.0 * offset * first + offset * offset * zeroth),
        factor * level_sum,
        factor * (slope_sum + offset * level_sum),
    )


def later(state, days):
    return shifted(state, math.exp(days * math.log(DECAY)), days / UNIT)


def weighted(state, weight, value, kernel):
    zeroth, first, second, level_sum, slope_sum = state
    product = weight * value
    return (
        zeroth + kernel[0] * weight,
        first + kernel[1] * weight,
        second + kernel[2] * weight,
        level_sum + kernel[0] * product,
        slope_sum + kernel[1] * product,
    )


def pack_body(count, share, days, chunks, me_ref, days_ref, anomaly, reliability, *refs):
    table, filled = refs[-2:]
    outs = refs[:-2]
    me = me_ref[0]
    for peer in range(count):
        filled[peer] = 0

    def place(index, carry):
        owner = days_ref[me * days + index] // days
        slot = filled[owner]
        filled[owner] = slot + 1
        table[owner * share + slot] = index
        return carry

    lax.fori_loop(0, days, place, 0)
    for peer in range(count):
        for slot in range(share):
            granule = table[(me ^ peer) * share + slot]
            for chunk, tiles in enumerate(chunks):
                out = outs[chunk * count + peer]
                for place_at, tile in enumerate(tiles):
                    rows = pl.ds(tile * TILE, TILE)
                    there = pl.ds(place_at * TILE, TILE)
                    out[slot, there, :] = anomaly[granule, rows, :]
                    out[share + slot, there, :] = reliability[granule, rows, :]


def plane_body(planes, inner, days, me_ref, table, kernels, anomaly, reliability, *outs):
    held = anomaly.shape[0] // planes
    rows, width = anomaly.shape[1:]
    part = width // inner
    lanes = min(LANES, part)
    me = me_ref[0] % inner
    for peer in range(inner):
        for tile in range(rows // TILE):
            for lane in range(part // lanes):
                here = pl.ds(tile * TILE, TILE)
                columns = pl.ds(pl.multiple_of((me ^ peer) * part + lane * lanes, lanes), lanes)
                zero = jnp.zeros((TILE, lanes), jnp.float32)
                state = (zero,) * 5
                for plane in range(planes - 1):
                    if plane:
                        state = later(state, inner * days)
                    for slot in range(held):
                        at = plane * held + slot
                        granule = table[at]
                        weight = reliability[granule, here, columns].astype(jnp.float32)
                        value = anomaly[granule, here, columns].astype(jnp.float32)
                        kernel = [kernels[power * anomaly.shape[0] + granule] for power in range(3)]
                        state = weighted(state, weight, value, kernel)
                    for field in range(5):
                        outs[peer][plane, field, here, lane * lanes : (lane + 1) * lanes] = state[field]


def total_body(count, share, positions, kernels, *refs):
    arrived = refs[:count]
    values, weights, total = refs[count:]
    rows, width = values.shape[1:]
    lanes = min(LANES, width)
    for peer in range(count):
        for slot in range(share):
            day = positions[peer * share + slot]
            values[day] = arrived[peer][slot]
            weights[day] = arrived[peer][share + slot]
    for tile in range(rows // TILE):
        here = pl.ds(tile * TILE, TILE)
        for lane in range(width // lanes):
            columns = slice(lane * lanes, (lane + 1) * lanes)
            zero = jnp.zeros((TILE, lanes), jnp.float32)
            state = (zero,) * 5
            for peer in range(count):
                for slot in range(share):
                    at = peer * share + slot
                    weight = arrived[peer][share + slot, here, columns].astype(jnp.float32)
                    value = arrived[peer][slot, here, columns].astype(jnp.float32)
                    kernel = [kernels[power * count * share + at] for power in range(3)]
                    state = weighted(state, weight, value, kernel)
            for field in range(5):
                total[field, here, columns] = state[field]


def begin(state_ref, inner, days, tiles, me_ref, shifts, prefixes, totals):
    width = state_ref.shape[2]
    part = width // inner
    me = me_ref[0] % inner
    for place_at, tile in enumerate(tiles):
        here = pl.ds(place_at * TILE, TILE)
        for peer in range(inner):
            columns = pl.ds(pl.multiple_of((me ^ peer) * part, part), part)
            state = tuple(prefixes[peer][field, tile * TILE : (tile + 1) * TILE, :] for field in range(5))
            state = shifted(state, shifts[0], shifts[1])
            for gap, block in enumerate(totals):
                extra = tuple(block[field, here, columns] for field in range(5))
                state = tuple(a + b for a, b in zip(state, later(extra, gap * days) if gap else extra))
            for field in range(5):
                state_ref[field, here, columns] = state[field]


def advance(state_ref, slopes, values, weights, ocean, tiles):
    steps, rows, width = slopes.shape
    lanes = min(LANES // 2, width)
    for place_at, tile in enumerate(tiles):
        here = pl.ds(place_at * TILE, TILE)
        for lane in range(width // lanes):
            columns = slice(lane * lanes, (lane + 1) * lanes)
            wet = ocean[tile * TILE : (tile + 1) * TILE, columns] > 0
            zeroth, first, second, level_sum, slope_sum = (
                state_ref[field, here, columns] for field in range(5)
            )
            for day in range(steps):
                weight = weights[day, here, columns].astype(jnp.float32)
                value = values[day, here, columns].astype(jnp.float32)
                second = DECAY * second + (2.0 * STEP * DECAY) * first + (STEP * STEP * DECAY) * zeroth
                first = DECAY * first + (STEP * DECAY) * zeroth
                zeroth = DECAY * zeroth + weight
                slope_sum = DECAY * slope_sum + (STEP * DECAY) * level_sum
                level_sum = DECAY * level_sum + weight * value
                det = zeroth * (second + RIDGE) - first * first
                slope = (first * level_sum - zeroth * slope_sum) / det
                slopes[day, here, columns] = jnp.where(wet, slope, 0.0)
            for field, moment in enumerate((zeroth, first, second, level_sum, slope_sum)):
                state_ref[field, here, columns] = moment


def lane_sum(rows):
    width = rows.shape[-1]
    column = lax.broadcasted_iota(jnp.int32, rows.shape, rows.ndim - 1)
    left = jnp.where(column > 0, pltpu.roll(rows, 1, rows.ndim - 1), 0.0)
    right = jnp.where(column < width - 1, pltpu.roll(rows, width - 1, rows.ndim - 1), 0.0)
    return left + rows + right


def edge_body(inner, days, tiles, me_ref, shifts, ocean, values, weights, *refs):
    prefixes, totals = refs[:inner], refs[inner : 2 * inner - 1]
    sums, top, bottom, state_ref, slopes = refs[2 * inner - 1 :]
    step = pl.program_id(0)
    steps = slopes.shape[0]

    @pl.when(step == 0)
    def _():
        begin(state_ref, inner, days, tiles, me_ref, shifts, prefixes, totals)
        land = lane_sum(ocean[...].astype(jnp.float32))
        top[days : days + 1, :] = land[:1]
        bottom[days : days + 1, :] = land[-1:]

    advance(state_ref, slopes, values, weights, ocean, tiles)
    for day in range(steps):
        around = lane_sum(slopes[day])
        sums[day] = around
        top[pl.ds(step * steps + day, 1), :] = around[:1]
        bottom[pl.ds(step * steps + day, 1), :] = around[-1:]


def stacked(upper, middle, lower, above, below):
    whole = jnp.concatenate([upper, middle, lower], axis=0)
    rows = whole.shape[0]
    row = lax.broadcasted_iota(jnp.int32, whole.shape, 0)
    before = jnp.where(row > 0, pltpu.roll(whole, 1, 0), above)
    after = jnp.where(row < rows - 1, pltpu.roll(whole, rows - 1, 0), below)
    return before + whole + after


def final_body(inner, days, tiles, me_ref, shifts, ocean, values, weights, sums, above, below, *refs):
    prefixes, totals = refs[:inner], refs[inner : 2 * inner - 1]
    trend, state_ref, slopes, scale = refs[2 * inner - 1 :]
    step = pl.program_id(0)
    steps = slopes.shape[0]

    @pl.when(step == 0)
    def _():
        begin(state_ref, inner, days, tiles, me_ref, shifts, prefixes, totals)
        land = lane_sum(ocean[...].astype(jnp.float32))
        count = stacked(
            land[:TILE],
            land[TILE:-TILE],
            land[-TILE:],
            above[days : days + 1, :],
            below[days : days + 1, :],
        )
        scale[...] = 1.0 / jnp.maximum(count, 1.0)

    advance(state_ref, slopes, values, weights, ocean, tiles)
    for day in range(steps):
        at = pl.ds(step * steps + day, 1)
        total = stacked(
            sums[day, :TILE], lane_sum(slopes[day]), sums[day, TILE:], above[at, :], below[at, :]
        )
        trend[day] = total * scale[...]


def on_device(ocean_heat_anomaly, observation_reliability, swath_date_number, marine_cell_flag):
    count = lax.axis_size("tm")
    tile_devices = lax.axis_size("tile")
    me = lax.axis_index("tm").astype(jnp.int32)
    days, rows, width = ocean_heat_anomaly.shape
    share = days // count
    inner = 1 << (count.bit_length() - 1) // 2
    planes = count // inner
    tiles = rows // TILE
    chunks = ((0, tiles - 1), tuple(range(1, tiles - 1)))
    me_ref = me.reshape(1)
    f32, bf16 = jnp.float32, jnp.bfloat16
    shape = jax.ShapeDtypeStruct

    *packed, table = pl.pallas_call(
        functools.partial(pack_body, count, share, days, chunks),
        name="pack",
        in_specs=[SMEM, SMEM, VMEM, VMEM],
        out_specs=[VMEM] * (2 * count) + [SMEM],
        out_shape=[
            shape((2 * share, len(part) * TILE, width), bf16) for part in chunks for _ in range(count)
        ]
        + [shape((days,), jnp.int32)],
        scratch_shapes=[pltpu.SMEM((count,), jnp.int32)],
    )(me_ref, swath_date_number, ocean_heat_anomaly, observation_reliability)

    arrived = []
    for chunk in range(2):
        own = packed[chunk * count]
        got = [own]
        for peer in range(count - 1, 0, -1):
            pairs = [(device, device ^ peer) for device in range(count)]
            got.insert(1, lax.ppermute(packed[chunk * count + peer], "tm", pairs))
        arrived.append(got)

    mine = lax.dynamic_slice_in_dim(swath_date_number, me * days, days)
    span = inner * days
    lag = ((span - 1) - mine % span).astype(f32)
    decay = jnp.exp(lag * math.log(DECAY))
    unit = lag / UNIT
    kernels = jnp.concatenate([decay, decay * unit, decay * unit * unit])
    part = width // inner
    planes_sent = pl.pallas_call(
        functools.partial(plane_body, planes, inner, days),
        name="plane",
        in_specs=[SMEM, SMEM, SMEM, VMEM, VMEM],
        out_specs=[VMEM] * inner,
        out_shape=[shape((planes - 1, 5, rows, part), f32)] * inner,
    )(me_ref, table, kernels, ocean_heat_anomaly, observation_reliability)
    sets = planes_sent[0]
    for peer in range(1, inner):
        sets = sets + lax.ppermute(
            planes_sent[peer], "tm", [(device, device ^ peer) for device in range(count)]
        )
    sets = [jnp.zeros_like(sets[0])] + [sets[index] for index in range(planes - 1)]
    bit = inner
    while len(sets) > 1:
        odd = (me & bit) > 0
        pairs = [(device, device ^ bit) for device in range(count)]
        keep = [jnp.where(odd, sets[index + 1], sets[index]) for index in range(0, len(sets), 2)]
        send = [jnp.where(odd, sets[index], sets[index + 1]) for index in range(0, len(sets), 2)]
        got = lax.ppermute(jnp.stack(send), "tm", pairs)
        sets = [keep[index] + got[index] for index in range(len(keep))]
        bit *= 2
    prefix = sets[0]
    prefixes = [prefix] + [
        lax.ppermute(prefix, "tm", [(device, device ^ peer) for device in range(count)])
        for peer in range(1, inner)
    ]

    owners = swath_date_number.reshape(count, days)
    match = owners // days == me
    rank = jnp.cumsum(match.astype(jnp.int32), axis=1) - 1
    slots = jnp.arange(share, dtype=jnp.int32)
    chosen = match[:, None, :] & (rank[:, None, :] == slots[None, :, None])
    position = jnp.sum(jnp.where(chosen, (owners % days)[:, None, :], 0), axis=2)
    order = jnp.arange(count, dtype=jnp.int32) ^ me
    pick = order[:, None] == jnp.arange(count, dtype=jnp.int32)[None, :]
    position = jnp.sum(jnp.where(pick[:, :, None], position[None], 0), axis=1).reshape(days)
    lag = ((days - 1) - position).astype(f32)
    decay = jnp.exp(lag * math.log(DECAY))
    unit = lag / UNIT
    kernels = jnp.concatenate([decay, decay * unit, decay * unit * unit])
    ahead = ((me % inner) * days).astype(f32)
    shifts = jnp.stack([jnp.exp(ahead * math.log(DECAY)), ahead / UNIT])

    sorted_chunks, neighbours = [], []
    for chunk, chunk_tiles in enumerate(chunks):
        height = len(chunk_tiles) * TILE
        values, weights, total = pl.pallas_call(
            functools.partial(total_body, count, share),
            name="total",
            in_specs=[SMEM, SMEM] + [VMEM] * count,
            out_specs=[VMEM] * 3,
            out_shape=[shape((days, height, width), bf16)] * 2 + [shape((5, height, width), f32)],
        )(position, kernels, *arrived[chunk])
        sorted_chunks.append((values, weights))
        neighbours.append(
            [
                lax.ppermute(
                    total,
                    "tm",
                    [(i, i + gap) for i in range(count) if i % inner + gap < inner],
                )
                for gap in range(1, inner)
            ]
        )

    step = TILE
    grid = (days // step,)
    whole = lambda *dims: pl.BlockSpec(dims, lambda t: (0,) * len(dims))
    by_day = lambda height: pl.BlockSpec((step, height, width), lambda t: (t, 0, 0))
    edge_height, mid_height = (len(part_tiles) * TILE for part_tiles in chunks)

    def state_specs(height):
        return [whole(5, rows, part)] * inner + [whole(5, height, width)] * (inner - 1)

    sums, top, bottom = pl.pallas_call(
        functools.partial(edge_body, inner, days, chunks[0]),
        name="edge",
        grid=grid,
        in_specs=[SMEM, SMEM, whole(rows, width), by_day(edge_height), by_day(edge_height)]
        + state_specs(edge_height),
        out_specs=[by_day(edge_height), whole(days + 1, width), whole(days + 1, width)],
        out_shape=[shape((days, edge_height, width), f32)] + [shape((days + 1, width), f32)] * 2,
        scratch_shapes=[
            pltpu.VMEM((5, edge_height, width), f32),
            pltpu.VMEM((step, edge_height, width), f32),
        ],
    )(me_ref, shifts, marine_cell_flag, *sorted_chunks[0], *prefixes, *neighbours[0])
    above = lax.ppermute(bottom, "tile", [(i, i + 1) for i in range(tile_devices - 1)])
    below = lax.ppermute(top, "tile", [(i + 1, i) for i in range(tile_devices - 1)])
    return pl.pallas_call(
        functools.partial(final_body, inner, days, chunks[1]),
        name="final",
        grid=grid,
        in_specs=[
            SMEM,
            SMEM,
            whole(rows, width),
            by_day(mid_height),
            by_day(mid_height),
            by_day(edge_height),
            whole(days + 1, width),
            whole(days + 1, width),
        ]
        + state_specs(mid_height),
        out_specs=by_day(rows),
        out_shape=shape((days, rows, width), f32),
        scratch_shapes=[
            pltpu.VMEM((5, mid_height, width), f32),
            pltpu.VMEM((step, mid_height, width), f32),
            pltpu.VMEM((rows, width), f32),
        ],
    )(me_ref, shifts, marine_cell_flag, *sorted_chunks[1], sums, above, below, *prefixes, *neighbours[1])


def solution(mesh):
    in_specs = (P("tm", "tile", None), P("tm", "tile", None), P(), P("tile", None))
    out_specs = P("tm", "tile", None)
    return jax.shard_map(
        on_device, mesh=mesh, in_specs=in_specs, out_specs=out_specs, check_vma=False
    )
```
